32 devices in a mesh: col: 8 (over z, x), tile: 4 (over y, core).
Axes of the slice: x: 2, y: 2, z: 4, core: 2. Of those that a mesh axis runs over, the one named last changes fastest.
Arguments:
- initial_image: float32 [16384, 1024], P('tile', 'col'), may hold values from -6 to 6
- panels: float32 [8, 256, 16384], P('col', None, 'tile'), may hold values from -0.046875 to 0.046875
- sinogram: float32 [8, 256, 1024], P(None, 'tile', 'col'), may hold values from -6 to 6
- subset_order: int32 [3], replicated, may hold values from 0 to 7
- step_sizes: float32 [3], replicated, may hold values from 0.5 to 1
Outputs:
- final_image: float32 [16384, 1024], P('tile', 'col')
- final_duals: float32 [8, 256, 1024], P(None, 'tile', 'col')
The draws below stay inside these ranges and needn't reach their ends.
Inputs may be any that keep to these rules, and one draw needn't show every extreme that they name: `subset_order`: repeats may occur.
All inputs are finite; a program needn't handle non-finite values.
Results may differ from the reference program's by a relative error of at most 0.00013.
Values sent between devices are 32-bit elements; how exact they have to be, the bound alone decides.
No kernel may reach another device: no remote copies, remote signals or barrier semaphores. Data moves between devices by JAX's collectives and lax.ppermute only.
A program may use at most 128 MiB of HBM per device.

```python
import jax
import jax.numpy as jnp
from jax import lax

WIDTH = 512
RSUB = 256
ITERS = 3
ROWS = 32
NPIX = 16384
CHANNELS = 1024
SUBSETS = 8


def block_levels(rng, shape, split, least, largest):
    gain = 1.0
    for axis_at, blocks in split:
        heights = jax.random.uniform(jax.random.fold_in(jax.random.fold_in(rng, 6), axis_at), (blocks,), jnp.float32, least / len(split), largest / len(split))
        gain = gain * jnp.repeat(jnp.exp(heights), shape[axis_at] // blocks).reshape((-1,) + (1,) * (len(shape) - 1 - axis_at))
    return gain


def scatter_about(key, dims, deviation, bound, pieces=(), kind=jnp.bfloat16):
    result = deviation * jax.random.normal(key, dims, jnp.float32)
    if pieces:
        result = result * block_levels(key, dims, pieces, -0.22, 0.18)
    return jnp.clip(result, -bound, bound).astype(kind)


def setup_inputs(seed: int = 0) -> dict:
    seeds = jax.random.split(jax.random.key(seed), 6)
    return {
        "initial_image": scatter_about(seeds[0], (NPIX, CHANNELS), 1.0, 6.0, ((0, 4), (1, 8)), jnp.float32),
        "panels": scatter_about(seeds[1], (SUBSETS, RSUB, NPIX), NPIX ** -0.5, 0.046875, ((0, 8), (2, 4)), jnp.float32),
        "sinogram": scatter_about(seeds[2], (SUBSETS, RSUB, CHANNELS), 1.0, 6.0, ((1, 4), (2, 8)), jnp.float32),
        "subset_order": jax.random.randint(seeds[3], (ITERS,), 0, SUBSETS).astype(jnp.int32),
        "step_sizes": jnp.clip(jax.random.uniform(seeds[4], (3,), jnp.float32, 0.5, 1.0), 0.5, 1.0),
    }


penalty = 0.2
smoothing = 1.0

def divergence(image_field):
    channels = image_field.shape[2]
    row_zero = jnp.zeros((1, WIDTH, channels), image_field.dtype)
    column_zero = jnp.zeros((image_field.shape[0], 1, channels), image_field.dtype)
    downward = jnp.concatenate([image_field[1:] - image_field[:-1], row_zero], axis=0)
    across = jnp.concatenate([image_field[:, 1:] - image_field[:, :-1], column_zero], axis=1)
    magnitude = jnp.sqrt(across * across + downward * downward + smoothing * smoothing)
    flux_across = across / magnitude
    flux_down = downward / magnitude
    shifted_across = jnp.concatenate([column_zero, flux_across[:, :-1]], axis=1)
    shifted_down = jnp.concatenate([row_zero, flux_down[:-1]], axis=0)
    return flux_across - shifted_across + flux_down - shifted_down

def reference(initial_image, panels, sinogram, subset_order, step_sizes):
    dual_step = step_sizes[0]
    primal_step = step_sizes[1]
    extrapolate = step_sizes[2]

    def primal(estimate, extrapolated):
        field_div = divergence(estimate.reshape(ROWS, WIDTH, CHANNELS)).reshape(estimate.shape)
        return estimate - primal_step * extrapolated + primal_step * penalty * field_div
    estimate = initial_image
    dual_state = jnp.zeros(sinogram.shape, jnp.float32)
    accumulated = jnp.zeros(initial_image.shape, jnp.float32)
    extrapolated = jnp.zeros(initial_image.shape, jnp.float32)
    for iteration in range(ITERS):
        estimate = primal(estimate, extrapolated)
        subset = subset_order[iteration].astype(jnp.int32)
        operator_panel = lax.dynamic_index_in_dim(panels, subset, 0, keepdims=False)
        forward = jnp.dot(operator_panel, estimate, precision=lax.Precision.HIGHEST, preferred_element_type=jnp.float32)
        current = lax.dynamic_index_in_dim(dual_state, subset, 0, keepdims=False)
        measured = lax.dynamic_index_in_dim(sinogram, subset, 0, keepdims=False)
        updated = (current + dual_step * forward - dual_step * measured) / (1.0 + dual_step)
        change = updated - current
        dual_state = lax.dynamic_update_index_in_dim(dual_state, updated, subset, 0)
        adjoint = jnp.dot(operator_panel.T, change, precision=lax.Precision.HIGHEST, preferred_element_type=jnp.float32)
        accumulated = accumulated + adjoint
        extrapolated = accumulated + extrapolate * SUBSETS * adjoint
    final_image = primal(estimate, extrapolated)
    return (final_image, dual_state)
```

```python
import jax
import jax.numpy as jnp
from jax import lax
from jax.sharding import PartitionSpec as P

WIDTH = 512
ITERS = 3


penalty = 0.2
smoothing = 1.0

PRECISION = lax.Precision.HIGH


def shifted(value, axis, by):
    count = lax.axis_size(axis)
    pairs = [(i, i + by) for i in range(count) if 0 <= i + by < count]
    return lax.ppermute(value, axis, pairs)


def ring_order(count):
    return list(range(0, count, 2)) + list(range(1, count, 2))[::-1]


def halo(estimate):
    channels = estimate.shape[1]
    image_field = estimate.reshape(-1, WIDTH, channels)
    row_below = shifted(image_field[:1], "tile", -1)
    row_above = shifted(image_field[-1:], "tile", 1)
    return row_below, row_above


def divergence(estimate, halos, tile_index, total_rows):
    channels = estimate.shape[1]
    image_field = estimate.reshape(-1, WIDTH, channels)
    rows_local = image_field.shape[0]
    row_below, row_above = halos
    extended = jnp.concatenate([row_above, image_field, row_below], axis=0)
    current = extended[:-1]
    downward = extended[1:] - current
    global_row = tile_index * rows_local - 1 + lax.broadcasted_iota(jnp.int32, (rows_local + 1, 1, 1), 0)
    inside = (global_row >= 0) & (global_row < total_rows - 1)
    downward = jnp.where(inside, downward, jnp.zeros_like(downward))
    column_zero = jnp.zeros((rows_local + 1, 1, channels), estimate.dtype)
    across = jnp.concatenate([current[:, 1:] - current[:, :-1], column_zero], axis=1)
    magnitude = jnp.sqrt(across * across + downward * downward + smoothing * smoothing)
    flux_across = (across / magnitude)[1:]
    flux_down = downward / magnitude
    shifted_across = jnp.concatenate([column_zero[1:], flux_across[:, :-1]], axis=1)
    field_div = flux_across - shifted_across + flux_down[1:] - flux_down[:-1]
    return field_div.reshape(estimate.shape)


def tile_sum(value):
    count = lax.axis_size("tile")
    step = 1
    while step < count:
        value = value + lax.ppermute(value, "tile", [(i, i ^ step) for i in range(count)])
        step *= 2
    return value


def gather_panels(panels, subset_order):
    count = lax.axis_size("col")
    stored, rays, pixels = panels.shape
    block = rays // count
    order = ring_order(count)
    cw = [(order[i], order[(i + 1) % count]) for i in range(count)]
    ccw = [(b, a) for a, b in cw]
    position_of = [order.index(i) for i in range(count)]
    mine = jnp.asarray(position_of, jnp.int32)[lax.axis_index("col")]
    order = jnp.asarray(order, jnp.int32)

    pieces = panels.reshape(stored, count, block, pixels)
    spread = lax.all_to_all(pieces, "col", split_axis=1, concat_axis=0, tiled=True)
    spread = spread.reshape(count * stored, block, pixels)

    gathered = []
    history = []
    for k in range(ITERS):
        chunk = lax.dynamic_index_in_dim(spread, subset_order[k], 0, keepdims=False)
        if len(history) >= 2:
            chunk, _ = lax.optimization_barrier((chunk, history[-2]))
        whole = jnp.zeros((rays, pixels), jnp.float32)

        def place(whole, piece, distance):
            owner = order[(mine + distance + count) % count]
            return lax.dynamic_update_slice(whole, piece, (owner * block, 0))

        whole = place(whole, chunk, 0)
        forwards, backwards = chunk, chunk
        for step in range(1, count // 2 + 1):
            forwards = lax.ppermute(forwards, "col", cw)
            whole = place(whole, forwards, -step)
            if step < count - step:
                backwards = lax.ppermute(backwards, "col", ccw)
                whole = place(whole, backwards, step)
            history.append((forwards, backwards))
        gathered.append(whole)
    return gathered


def per_device(initial_image, panels, sinogram, subset_order, step_sizes):
    dual_step = step_sizes[0]
    primal_step = step_sizes[1]
    extrapolate = step_sizes[2]
    tile_count = lax.axis_size("tile")
    tile_index = lax.axis_index("tile")
    total_rows = initial_image.shape[0] // WIDTH * tile_count
    rays_local = panels.shape[1] // tile_count
    subset_count = sinogram.shape[0]

    def base_of(estimate):
        field_div = divergence(estimate, halo(estimate), tile_index, total_rows)
        return lax.optimization_barrier(estimate + primal_step * penalty * field_div)

    operator_panels = gather_panels(panels, subset_order)
    measured_own = jnp.stack([lax.dynamic_index_in_dim(sinogram, subset_order[k], 0, keepdims=False) for k in range(ITERS)])
    measured = lax.all_gather(measured_own, "tile", axis=1, tiled=True)

    estimate = base_of(initial_image)
    duals = []
    dual_state = jnp.zeros(sinogram.shape, jnp.float32)
    accumulated = jnp.zeros(initial_image.shape, jnp.float32)
    for k in range(ITERS):
        operator_panel = operator_panels[k]
        forward = tile_sum(
            jnp.dot(operator_panel, estimate, precision=PRECISION, preferred_element_type=jnp.float32)
        )
        base = base_of(estimate)
        current = jnp.zeros_like(forward)
        for j in range(k):
            current = jnp.where(subset_order[j] == subset_order[k], duals[j], current)
        updated = (current + dual_step * forward - dual_step * measured[k]) / (1.0 + dual_step)
        change = updated - current
        duals.append(updated)
        adjoint = lax.dot_general(
            operator_panel,
            change,
            (((0,), (0,)), ((), ())),
            precision=PRECISION,
            preferred_element_type=jnp.float32,
        )
        mine = lax.dynamic_slice_in_dim(updated, tile_index * rays_local, rays_local, 0)
        dual_state = lax.dynamic_update_index_in_dim(dual_state, mine, subset_order[k], 0)
        accumulated = accumulated + adjoint
        extrapolated = accumulated + extrapolate * subset_count * adjoint
        estimate = base - primal_step * extrapolated
    return (estimate, dual_state)


def solution(mesh):
    in_specs = (P("tile", "col"), P("col", None, "tile"), P(None, "tile", "col"), P(), P())
    out_specs = (P("tile", "col"), P(None, "tile", "col"))
    return jax.shard_map(
        per_device, mesh=mesh, in_specs=in_specs, out_specs=out_specs, check_vma=False
    )
```

```python
import jax
import jax.numpy as jnp
from jax import lax
from jax.sharding import PartitionSpec as P


WIDTH = 512
ITERS = 3


penalty = 0.2
smoothing = 1.0

PRECISION = lax.Precision.HIGH
PIECES = 4


def shifted(value, axis, by):
    count = lax.axis_size(axis)
    pairs = [(i, i + by) for i in range(count) if 0 <= i + by < count]
    return lax.ppermute(value, axis, pairs)


def halo(estimate):
    channels = estimate.shape[1]
    image_field = estimate.reshape(-1, WIDTH, channels)
    row_below = shifted(image_field[:1], "tile", -1)
    row_above = shifted(image_field[-1:], "tile", 1)
    return row_below, row_above


def divergence(estimate, halos, tile_index, total_rows):
    channels = estimate.shape[1]
    image_field = estimate.reshape(-1, WIDTH, channels)
    rows_local = image_field.shape[0]
    row_below, row_above = halos
    extended = jnp.concatenate([row_above, image_field, row_below], axis=0)
    current = extended[:-1]
    downward = extended[1:] - current
    global_row = tile_index * rows_local - 1 + lax.broadcasted_iota(jnp.int32, (rows_local + 1, 1, 1), 0)
    inside = (global_row >= 0) & (global_row < total_rows - 1)
    downward = jnp.where(inside, downward, jnp.zeros_like(downward))
    column_zero = jnp.zeros((rows_local + 1, 1, channels), estimate.dtype)
    across = jnp.concatenate([current[:, 1:] - current[:, :-1], column_zero], axis=1)
    magnitude = jnp.sqrt(across * across + downward * downward + smoothing * smoothing)
    flux_across = (across / magnitude)[1:]
    flux_down = downward / magnitude
    shifted_across = jnp.concatenate([column_zero[1:], flux_across[:, :-1]], axis=1)
    field_div = flux_across - shifted_across + flux_down[1:] - flux_down[:-1]
    return field_div.reshape(estimate.shape)


def tile_sum(value):
    count = lax.axis_size("tile")
    step = 1
    while step < count:
        value = value + lax.ppermute(value, "tile", [(i, i ^ step) for i in range(count)])
        step *= 2
    return value


def exchange(value, bit):
    count = lax.axis_size("col")
    return lax.ppermute(value, "col", [(i, i ^ bit) for i in range(count)])


def block_bits(group):
    bits = []
    bit = group // 2
    while bit:
        bits.append(bit)
        bit //= 2
    return bits


def to_arrival_order(rows, group, mine, axis):
    lead = rows.shape[:axis]
    tail = rows.shape[axis + 1 :]
    bits = block_bits(group)
    block = rows.shape[axis] // group
    rows = rows.reshape(lead + (2,) * len(bits) + (PIECES, block // PIECES) + tail)
    for at, bit in enumerate(bits):
        flip = (mine & bit) != 0
        rows = jnp.where(flip, jnp.flip(rows, axis + at), rows)
    order = list(range(axis))
    order += [axis + len(bits)]
    order += [axis + at for at in reversed(range(len(bits)))]
    order += list(range(axis + len(bits) + 1, rows.ndim))
    return rows.transpose(order).reshape(lead + (-1,) + tail)


def from_arrival_order(rows, group, mine):
    tail = rows.shape[1:]
    bits = block_bits(group)
    total = rows.shape[0]
    rows = rows.reshape((PIECES,) + (2,) * len(bits) + (total // group // PIECES,) + tail)
    order = [1 + at for at in reversed(range(len(bits)))] + [0]
    order += list(range(len(bits) + 1, rows.ndim))
    rows = rows.transpose(order)
    for at, bit in enumerate(bits):
        flip = (mine & bit) != 0
        rows = jnp.where(flip, jnp.flip(rows, at), rows)
    return rows.reshape((total,) + tail)


def spread_panels(panels, group):
    stored, rays, pixels = panels.shape
    sub = rays // group // PIECES
    mine = lax.axis_index("col") & (group - 1)
    spread = []
    for piece in range(PIECES):
        blocks = panels.reshape(stored, group, PIECES, sub, pixels)
        parts = [
            lax.dynamic_slice(
                blocks, (0, mine ^ bit, piece, 0, 0), (stored, 1, 1, sub, pixels), allow_negative_indices=False
            ).reshape(stored, sub, pixels)
            for bit in range(group)
        ]
        parts, panels = lax.optimization_barrier((parts, panels))
        for bit in range(1, group):
            parts[bit] = exchange(parts[bit], bit)
        spread.append(parts)
    return spread


def choose(parts, wanted, local):
    near = None
    for bit, part in enumerate(parts):
        held = part[0]
        for at in range(1, part.shape[0]):
            held = jnp.where(local == at, part[at], held)
        near = held if near is None else jnp.where(wanted == bit, held, near)
    return near


def rows_of(values, width):
    return lax.optimization_barrier(jnp.broadcast_to(values.reshape(-1, 1), (values.size, width)))


def gather_panels(panels, subset_order):
    group = lax.axis_size("col") // 2
    stored, _, pixels = panels.shape
    me = lax.axis_index("col")
    spread = spread_panels(panels, group)
    bits = block_bits(group)
    owner = rows_of(lax.div(subset_order, jnp.int32(stored)) ^ me, pixels)
    local = rows_of(lax.rem(subset_order, jnp.int32(stored)), pixels) if stored > 1 else None
    arrived = []
    for k in range(ITERS):
        distance = owner[k : k + 1]
        place = None if local is None else local[k : k + 1]
        for piece in range(PIECES):
            parts, apart = lax.optimization_barrier((spread[piece], distance))
            near = choose(parts, apart & (group - 1), place)
            near, apart = lax.optimization_barrier((near, distance))
            far = exchange(near, group)
            known = jnp.where(apart < group, near, far)
            known = lax.optimization_barrier(known)
            parts = [known]
            for at, bit in enumerate(bits):
                other = exchange(known, bit)
                parts.append(other)
                if at + 1 < len(bits):
                    known = jnp.concatenate([known, other], axis=0)
                    known = lax.optimization_barrier(known)
            arrived.append(parts)
    gathered = []
    for k in range(ITERS):
        parts = sum(arrived[k * PIECES : (k + 1) * PIECES], [])
        gathered.append(jnp.concatenate(lax.optimization_barrier(parts), axis=0))
    return gathered


def per_device(initial_image, panels, sinogram, subset_order, step_sizes):
    channels = initial_image.shape[1]
    dual_step, primal_step, extrapolate = jnp.split(rows_of(step_sizes, channels), 3)
    chosen = [row[None] for row in jnp.split(rows_of(subset_order, channels), ITERS)]
    tile_count = lax.axis_size("tile")
    tile_index = lax.axis_index("tile")
    total_rows = initial_image.shape[0] // WIDTH * tile_count
    rays_local = panels.shape[1] // tile_count
    subset_count = sinogram.shape[0]
    group = lax.axis_size("col") // 2
    mine = lax.axis_index("col") & (group - 1)

    def base_of(estimate):
        field_div = divergence(estimate, halo(estimate), tile_index, total_rows)
        return lax.optimization_barrier(estimate + primal_step * penalty * field_div)

    operator_panels = gather_panels(panels, subset_order)
    subset_at = lax.broadcasted_iota(jnp.int32, (subset_count, 1, 1), 0)
    measured = jnp.stack([jnp.sum(jnp.where(subset_at == chosen[k], sinogram, 0.0), axis=0) for k in range(ITERS)])
    everywhere = jnp.zeros((ITERS, panels.shape[1], sinogram.shape[2]), jnp.float32)
    measured = lax.dynamic_update_slice(everywhere, measured, (0, tile_index * rays_local, 0), allow_negative_indices=False)
    measured = to_arrival_order(measured, group, mine, 1)

    estimate = base_of(initial_image)
    duals = []
    dual_state = jnp.zeros(sinogram.shape, jnp.float32)
    accumulated = jnp.zeros(initial_image.shape, jnp.float32)
    for k in range(ITERS):
        operator_panel = operator_panels[k]
        residual = tile_sum(
            jnp.dot(operator_panel, estimate, precision=PRECISION, preferred_element_type=jnp.float32)
            - measured[k]
        )
        base = base_of(estimate)
        current = jnp.zeros_like(residual)
        for j in range(k):
            current = jnp.where(chosen[j][0] == chosen[k][0], duals[j], current)
        updated = (current + dual_step * residual) / (1.0 + dual_step)
        change = updated - current
        duals.append(updated)
        adjoint = lax.dot_general(
            operator_panel,
            change,
            (((0,), (0,)), ((), ())),
            precision=PRECISION,
            preferred_element_type=jnp.float32,
        )
        ordered = from_arrival_order(updated, group, mine)
        own_rays = lax.dynamic_slice_in_dim(ordered, tile_index * rays_local, rays_local, 0, allow_negative_indices=False)
        dual_state = jnp.where(subset_at == chosen[k], own_rays[None], dual_state)
        accumulated = accumulated + adjoint
        extrapolated = accumulated + extrapolate * subset_count * adjoint
        estimate = base - primal_step * extrapolated
    return (estimate, dual_state)


def solution(mesh):
    in_specs = (P("tile", "col"), P("col", None, "tile"), P(None, "tile", "col"), P(), P())
    out_specs = (P("tile", "col"), P(None, "tile", "col"))

    return jax.shard_map(per_device, mesh=mesh, in_specs=in_specs, out_specs=out_specs, check_vma=False)
```

```python
import jax
import jax.numpy as jnp
from jax import lax
from jax.experimental import pallas as pl
from jax.experimental.pallas import tpu as pltpu
from jax.sharding import PartitionSpec as P


WIDTH = 512
ITERS = 3


penalty = 0.2
smoothing = 1.0

PRECISION = lax.Precision.HIGH
PIECES = 4
SPLIT = ((4,), (4,), (3, 1))


def shifted(value, axis, by):
    count = lax.axis_size(axis)
    pairs = [(i, i + by) for i in range(count) if 0 <= i + by < count]
    return lax.ppermute(value, axis, pairs)


def halo(estimate):
    channels = estimate.shape[1]
    image_field = estimate.reshape(-1, WIDTH, channels)
    row_below = shifted(image_field[:1], "tile", -1)
    row_above = shifted(image_field[-1:], "tile", 1)
    return row_below, row_above


def smoothed(estimate, halos, edges, weight):
    channels = estimate.shape[1]
    image_field = estimate.reshape(-1, WIDTH, channels)
    rows = image_field.shape[0]

    def fluxes(here, below):
        down = below - here
        ahead = pltpu.roll(here, WIDTH - 1, 0)
        column = lax.broadcasted_iota(jnp.int32, (WIDTH, channels), 0)
        across = jnp.where(column < WIDTH - 1, ahead - here, 0.0)
        return across, down, column

    def kernel(field_ref, below_ref, above_ref, edges_ref, weight_ref, out_ref):
        def scale(across, down):
            return lax.rsqrt(across * across + down * down + smoothing * smoothing)

        above = above_ref[0]
        across, down, _ = fluxes(above, field_ref[0])
        down = down * edges_ref[0:1, :]
        before = down * scale(across, down)

        def row(at, before):
            here = field_ref[at]
            last = at == rows - 1
            below = jnp.where(last, below_ref[0], field_ref[jnp.minimum(at + 1, rows - 1)])
            across, down, column = fluxes(here, below)
            down = down * jnp.where(last, edges_ref[1:2, :], 1.0)
            inverse = scale(across, down)
            across, down = across * inverse, down * inverse
            behind = jnp.where(column > 0, pltpu.roll(across, 1, 0), 0.0)
            out_ref[at] = here + weight_ref[...] * (across - behind + down - before)
            return down

        lax.fori_loop(0, rows, row, before)

    vmem = pl.BlockSpec(memory_space=pltpu.VMEM)
    return pl.pallas_call(
        kernel,
        in_specs=[vmem] * 5,
        out_specs=vmem,
        out_shape=jax.ShapeDtypeStruct(image_field.shape, jnp.float32),
        compiler_params=pltpu.CompilerParams(vmem_limit_bytes=16 * estimate.size),
        cost_estimate=pl.CostEstimate(
            flops=20 * estimate.size, bytes_accessed=8 * estimate.size, transcendentals=estimate.size
        ),
    )(image_field, *halos, edges, weight).reshape(estimate.shape)


def tile_sum(value):
    count = lax.axis_size("tile")
    step = 1
    while step < count:
        value = value + lax.ppermute(value, "tile", [(i, i ^ step) for i in range(count)])
        step *= 2
    return value


def exchange(value, bit):
    count = lax.axis_size("col")
    return lax.ppermute(value, "col", [(i, i ^ bit) for i in range(count)])


def block_bits(group):
    bits = []
    bit = group // 2
    while bit:
        bits.append(bit)
        bit //= 2
    return bits


def to_arrival_order(rows, group, mine, axis):
    lead = rows.shape[:axis]
    tail = rows.shape[axis + 1 :]
    bits = block_bits(group)
    block = rows.shape[axis] // group
    rows = rows.reshape(lead + (2,) * len(bits) + (PIECES, block // PIECES) + tail)
    for at, bit in enumerate(bits):
        flip = (mine & bit) != 0
        rows = jnp.where(flip, jnp.flip(rows, axis + at), rows)
    order = list(range(axis))
    order += [axis + len(bits)]
    order += [axis + at for at in reversed(range(len(bits)))]
    order += list(range(axis + len(bits) + 1, rows.ndim))
    return rows.transpose(order).reshape(lead + (-1,) + tail)


def from_arrival_order(rows, group, mine):
    tail = rows.shape[1:]
    bits = block_bits(group)
    total = rows.shape[0]
    rows = rows.reshape((PIECES,) + (2,) * len(bits) + (total // group // PIECES,) + tail)
    order = [1 + at for at in reversed(range(len(bits)))] + [0]
    order += list(range(len(bits) + 1, rows.ndim))
    rows = rows.transpose(order)
    for at, bit in enumerate(bits):
        flip = (mine & bit) != 0
        rows = jnp.where(flip, jnp.flip(rows, at), rows)
    return rows.reshape((total,) + tail)


def spread_panels(panels, group):
    stored, rays, pixels = panels.shape
    sub = rays // group // PIECES
    mine = lax.axis_index("col") & (group - 1)
    spread = []
    for piece in range(PIECES):
        blocks = panels.reshape(stored, group, PIECES, sub, pixels)
        parts = [
            lax.dynamic_slice(
                blocks, (0, mine ^ bit, piece, 0, 0), (stored, 1, 1, sub, pixels), allow_negative_indices=False
            ).reshape(stored, sub, pixels)
            for bit in range(group)
        ]
        parts, panels = lax.optimization_barrier((parts, panels))
        for bit in sorted(range(1, group), key=lambda bit: (bit ^ (group // 2))):
            parts[bit] = exchange(parts[bit], bit)
        spread.append(parts)
    return spread


def choose(parts, wanted, local):
    near = None
    for bit, part in enumerate(parts):
        held = part[0]
        for at in range(1, part.shape[0]):
            held = jnp.where(local == at, part[at], held)
        near = held if near is None else jnp.where(wanted == bit, held, near)
    return near


def rows_of(values, width):
    return lax.optimization_barrier(jnp.broadcast_to(values.reshape(-1, 1), (values.size, width)))


def gather_panels(panels, subset_order):
    group = lax.axis_size("col") // 2
    stored, _, pixels = panels.shape
    me = lax.axis_index("col")
    spread = spread_panels(panels, group)
    bits = block_bits(group)
    owner = rows_of(lax.div(subset_order, jnp.int32(stored)) ^ me, pixels)
    local = rows_of(lax.rem(subset_order, jnp.int32(stored)), pixels) if stored > 1 else None
    arrived = []
    for k in range(ITERS):
        distance = owner[k : k + 1]
        place = None if local is None else local[k : k + 1]
        for piece in range(PIECES):
            parts, apart = lax.optimization_barrier((spread[piece], distance))
            near = choose(parts, apart & (group - 1), place)
            near, apart = lax.optimization_barrier((near, distance))
            far = exchange(near, group)
            known = jnp.where(apart < group, near, far)
            known = lax.optimization_barrier(known)
            parts = [known]
            for at, bit in enumerate(bits):
                other = exchange(known, bit)
                parts.append(other)
                if at + 1 < len(bits):
                    known = jnp.concatenate([known, other], axis=0)
                    known = lax.optimization_barrier(known)
            arrived.append(parts)
    gathered = []
    for k in range(ITERS):
        panel = []
        start = k * PIECES
        for size in SPLIT[k]:
            parts = sum(arrived[start : start + size], [])
            panel.append(jnp.concatenate(lax.optimization_barrier(parts), axis=0))
            start += size
        gathered.append(panel)
    return gathered


def per_device(initial_image, panels, sinogram, subset_order, step_sizes):
    channels = initial_image.shape[1]
    dual_step, primal_step, extrapolate = jnp.split(rows_of(step_sizes, channels), 3)
    chosen = [row[None] for row in jnp.split(rows_of(subset_order, channels), ITERS)]
    tile_count = lax.axis_size("tile")
    tile_index = lax.axis_index("tile")
    rays_local = panels.shape[1] // tile_count
    subset_count = sinogram.shape[0]
    group = lax.axis_size("col") // 2
    mine = lax.axis_index("col") & (group - 1)

    has_above = jnp.where(tile_index > 0, 1.0, 0.0)
    has_below = jnp.where(tile_index < tile_count - 1, 1.0, 0.0)
    edges = rows_of(jnp.stack([has_above, has_below]), channels)

    def base_of(estimate):
        return smoothed(estimate, halo(estimate), edges, primal_step * penalty)

    operator_panels = gather_panels(panels, subset_order)
    subset_at = lax.broadcasted_iota(jnp.int32, (subset_count, 1, 1), 0)
    measured = jnp.stack([jnp.sum(jnp.where(subset_at == chosen[k], sinogram, 0.0), axis=0) for k in range(ITERS)])
    everywhere = jnp.zeros((ITERS, panels.shape[1], sinogram.shape[2]), jnp.float32)
    measured = lax.dynamic_update_slice(everywhere, measured, (0, tile_index * rays_local, 0), allow_negative_indices=False)
    measured = to_arrival_order(measured, group, mine, 1)

    estimate = base_of(initial_image)
    duals = []
    dual_state = jnp.zeros(sinogram.shape, jnp.float32)
    accumulated = jnp.zeros(initial_image.shape, jnp.float32)
    for k in range(ITERS):
        base = base_of(estimate) - primal_step * accumulated if k else base_of(estimate)
        found = []
        start = 0
        for operator_panel in operator_panels[k]:
            rows = slice(start, start + operator_panel.shape[0])
            start += operator_panel.shape[0]
            residual = tile_sum(
                jnp.dot(operator_panel, estimate, precision=PRECISION, preferred_element_type=jnp.float32)
                - measured[k, rows]
            )
            current = jnp.zeros_like(residual)
            for j in range(k):
                current = jnp.where(chosen[j][0] == chosen[k][0], duals[j][rows], current)
            updated = (current + dual_step * residual) / (1.0 + dual_step)
            change = updated - current
            if k + 1 == ITERS:
                change = primal_step * (1.0 + extrapolate * subset_count) * change
            adjoint = lax.dot_general(
                operator_panel,
                change,
                (((0,), (0,)), ((), ())),
                precision=PRECISION,
                preferred_element_type=jnp.float32,
            )
            found.append(updated)
            if k + 1 == ITERS:
                base = base - adjoint
            else:
                base = base - primal_step * (1.0 + extrapolate * subset_count) * adjoint
                accumulated = accumulated + adjoint
            if start < panels.shape[1]:
                base = lax.optimization_barrier(base)
        duals.append(jnp.concatenate(found, axis=0))
        ordered = from_arrival_order(duals[k], group, mine)
        own_rays = lax.dynamic_slice_in_dim(ordered, tile_index * rays_local, rays_local, 0, allow_negative_indices=False)
        dual_state = jnp.where(subset_at == chosen[k], own_rays[None], dual_state)
        estimate = base
    return (estimate, dual_state)


def solution(mesh):
    in_specs = (P("tile", "col"), P("col", None, "tile"), P(None, "tile", "col"), P(), P())
    out_specs = (P("tile", "col"), P(None, "tile", "col"))

    return jax.shard_map(per_device, mesh=mesh, in_specs=in_specs, out_specs=out_specs, check_vma=False)
```
